32 devices in a mesh: wide: 16 (over z, x, core), head: 2 (over y).
Axes of the slice: x: 2, y: 2, z: 4, core: 2. Of those that a mesh axis runs over, the one named last changes fastest.
Arguments:
- queries: bfloat16 [8192, 8192], P(('wide', 'head')), may hold values from -6 to 6
- keys: bfloat16 [8192, 1024], P(('wide', 'head')), may hold values from -6 to 6
- values: bfloat16 [8192, 1024], P(('wide', 'head')), may hold values from -6 to 6
- out_rows: bfloat16 [8192, 8192], P(('wide', 'head')), may hold values from -3 to 3
- output_gradient: bfloat16 [8192, 8192], P(('wide', 'head')), may hold values from -3 to 3
- log_norm_rows: float32 [8192, 64], P(('wide', 'head')), may hold values from 4 to 8
- doc_lengths: int32 [16], replicated, may hold values from 1 to 768, 8192 in all
Outputs:
- q_grad: float32 [8192, 8192], P(('wide', 'head'))
- key_gradient: float32 [8192, 1024], P(('wide', 'head'))
- value_gradient: float32 [8192, 1024], P(('wide', 'head'))
The draws below stay inside these ranges and needn't reach their ends.
Inputs may be any that keep to these rules, and one draw needn't show every extreme that they name: `doc_lengths`: 16 document lengths in order; they sum to 8192.
All inputs are finite; a program needn't handle non-finite values.
Results may differ from the reference program's by a relative error of at most 0.0058.
Values may be sent and summed in bfloat16 or wider, within the bound.
A program may use at most 192 MiB of HBM per device.

```python
import math
import jax
import jax.numpy as jnp
import numpy as np
from jax import lax

QUERY_HEADS = 64
KEY_VALUE_HEADS = 8
HEAD_SIZE = 128
DOCS = 16
PACKED_TOKENS = 8192
DOC_MOST = 768


def steps_of(rng, extent, shards, low, top_value):
    level = 1.0
    for axis_at, parts in shards:
        heights = jax.random.uniform(jax.random.fold_in(jax.random.fold_in(rng, 6), axis_at), (parts,), jnp.float32, low / len(shards), top_value / len(shards))
        level = level * jnp.repeat(jnp.exp(heights), extent[axis_at] // parts).reshape((-1,) + (1,) * (len(extent) - 1 - axis_at))
    return level


def split_up(number_of, total, limit, lean):
    weights = [(1 << 20) // math.isqrt(rank ** lean) + 1 for rank in range(2, number_of + 1)]
    rest, counts = total - limit - (number_of - 1), [1] * (number_of - 1)
    while rest > 0:
        movable = [i for i in range(number_of - 1) if counts[i] < limit]
        pool, left = sum([weights[i] for i in movable]), rest
        for i in movable:
            extra = min(limit - counts[i], max(1, left * weights[i] // pool), rest)
            counts[i] = counts[i] + extra
            rest = rest - extra
    return np.array([limit] + counts)


def uneven_parts(key, count, total, most, lean):
    if count == 2:
        one = jax.random.randint(key, (), max(1, total - most), min(most, total - 1) + 1)
        return jnp.stack([one, total - one])
    lengths = jnp.asarray(split_up(count, total, most, lean), jnp.int32)
    twos = (count - 1) // 2
    source_of, sink = lengths[1:1 + 2 * twos:2], lengths[2:2 + 2 * twos:2]
    margin = jnp.minimum(source_of - 1, most - sink)
    shifted = jax.random.randint(jax.random.fold_in(key, 1), (twos,), 0, 1 << 20) % (margin + 1)
    lengths = lengths.at[1:1 + 2 * twos:2].set(source_of - shifted).at[2:2 + 2 * twos:2].set(sink + shifted)
    return lengths[jax.random.permutation(jax.random.fold_in(key, 2), count)]


def normal_values(rng, extent, width, most, shards=(), kind=jnp.bfloat16):
    values = width * jax.random.normal(rng, extent, jnp.float32)
    if shards:
        values = values * steps_of(rng, extent, shards, -0.22, 0.18)
    return jnp.clip(values, -most, most).astype(kind)


def setup_inputs(seed: int = 0) -> dict:
    key_list = jax.random.split(jax.random.key(seed), 8)
    queries = normal_values(key_list[0], (PACKED_TOKENS, QUERY_HEADS * HEAD_SIZE), 1.0, 6.0, ((0, 32),))
    keys = normal_values(key_list[1], (PACKED_TOKENS, KEY_VALUE_HEADS * HEAD_SIZE), 1.0, 6.0, ((0, 32),))
    values = normal_values(key_list[2], (PACKED_TOKENS, KEY_VALUE_HEADS * HEAD_SIZE), 1.0, 6.0, ((0, 32),))
    out_rows = normal_values(key_list[3], (PACKED_TOKENS, QUERY_HEADS * HEAD_SIZE), 0.5, 3.0, ((0, 32),))
    output_gradient = normal_values(key_list[4], (PACKED_TOKENS, QUERY_HEADS * HEAD_SIZE), 0.5, 3.0, ((0, 32),))
    log_norm_rows = jnp.clip(4.0 + 4.0 * jax.random.uniform(key_list[5], (PACKED_TOKENS, QUERY_HEADS), jnp.float32) ** steps_of(key_list[5], (PACKED_TOKENS, QUERY_HEADS), ((0, 32),), -0.2, 0.2), 4.0, 8.0)
    doc_lengths = uneven_parts(key_list[6], DOCS, PACKED_TOKENS, DOC_MOST, 2).astype(jnp.int32)
    return dict(queries=queries, keys=keys, values=values, out_rows=out_rows, output_gradient=output_gradient, log_norm_rows=log_norm_rows, doc_lengths=doc_lengths)


def doc_number(doc_lengths, positions):
    doc_ends = jnp.cumsum(doc_lengths)
    found = lax.optimization_barrier(jnp.sum((doc_ends[None, :] <= positions[:, None]).astype(jnp.int32), axis=1))
    return jnp.where(positions < 0, -1, found).astype(jnp.int32)

def pair_terms(query_rows, grad_rows, norm_rows, delta_rows, allowed, k_block, v_block, scaling):
    row_count = allowed.shape[0]
    key_count = k_block.shape[0]
    group_count = norm_rows.shape[1]
    forward_dims = (((1,), (1,)), ((), ()))
    backward_dims = (((0,), (0,)), ((), ()))
    scores = lax.dot_general(query_rows, k_block, forward_dims, preferred_element_type=jnp.float32)
    scores = scores.reshape(row_count, group_count, key_count)
    attend = jnp.where(allowed[:, None, :], jnp.exp(scores * scaling - norm_rows[:, :, None]), 0.0)
    prob_grad = lax.dot_general(grad_rows, v_block, forward_dims, preferred_element_type=jnp.float32)
    prob_grad = prob_grad.reshape(row_count, group_count, key_count)
    score_grad = attend * (prob_grad - delta_rows[:, :, None])
    attend_low = attend.astype(jnp.bfloat16).reshape(row_count * group_count, key_count)
    score_low = score_grad.astype(jnp.bfloat16).reshape(row_count * group_count, key_count)
    value_term = lax.dot_general(attend_low, grad_rows, backward_dims, preferred_element_type=jnp.float32)
    key_term = lax.dot_general(score_low, query_rows, backward_dims, preferred_element_type=jnp.float32)
    query_term = jnp.dot(score_low, k_block, preferred_element_type=jnp.float32)
    return (query_term, key_term, value_term)

def reference(queries, keys, values, out_rows, output_gradient, log_norm_rows, doc_lengths):
    every_row_set = queries.shape[0]
    group_count = QUERY_HEADS // KEY_VALUE_HEADS
    scaling = 1.0 / math.sqrt(HEAD_SIZE)
    delta_per_row = lax.optimization_barrier(jnp.sum((output_gradient.astype(jnp.float32) * out_rows.astype(jnp.float32)).reshape(every_row_set, QUERY_HEADS, HEAD_SIZE), axis=2))
    tile_rows = min(256, every_row_set)
    tile_count = every_row_set // tile_rows
    positions = jnp.arange(every_row_set, dtype=jnp.int32)
    doc_index = doc_number(doc_lengths, positions)
    query_per_head = queries.reshape(every_row_set, KEY_VALUE_HEADS, group_count * HEAD_SIZE).transpose(1, 0, 2)
    gradient_per_head = output_gradient.reshape(every_row_set, KEY_VALUE_HEADS, group_count * HEAD_SIZE).transpose(1, 0, 2)
    norm_per_head = log_norm_rows.reshape(every_row_set, KEY_VALUE_HEADS, group_count).transpose(1, 0, 2)
    delta_per_head = delta_per_row.reshape(every_row_set, KEY_VALUE_HEADS, group_count).transpose(1, 0, 2)
    key_per_head = keys.reshape(every_row_set, KEY_VALUE_HEADS, HEAD_SIZE).transpose(1, 0, 2)
    value_per_head = values.reshape(every_row_set, KEY_VALUE_HEADS, HEAD_SIZE).transpose(1, 0, 2)

    def one_head(operands):
        query_head, grad_head, norm_head, delta_head, key_head, value_head = operands

        def visit(pair_index, running):
            query_tile = (pair_index // tile_count).astype(jnp.int32)
            key_tile = (pair_index % tile_count).astype(jnp.int32)
            query_start = (query_tile * tile_rows).astype(jnp.int32)
            key_start = (key_tile * tile_rows).astype(jnp.int32)
            needed = (key_tile <= query_tile) & (doc_index[key_start + tile_rows - 1] >= doc_index[query_start])

            def compute(state):
                query_acc, key_acc, value_acc = state
                query_rows = lax.dynamic_slice_in_dim(query_head, query_start, tile_rows, 0).reshape(tile_rows * group_count, HEAD_SIZE)
                grad_rows = lax.dynamic_slice_in_dim(grad_head, query_start, tile_rows, 0).reshape(tile_rows * group_count, HEAD_SIZE)
                norm_rows = lax.dynamic_slice_in_dim(norm_head, query_start, tile_rows, 0)
                delta_rows = lax.dynamic_slice_in_dim(delta_head, query_start, tile_rows, 0)
                k_block = lax.dynamic_slice_in_dim(key_head, key_start, tile_rows, 0)
                v_block = lax.dynamic_slice_in_dim(value_head, key_start, tile_rows, 0)
                query_pos = lax.dynamic_slice_in_dim(positions, query_start, tile_rows, 0)
                key_pos = lax.dynamic_slice_in_dim(positions, key_start, tile_rows, 0)
                query_doc = lax.dynamic_slice_in_dim(doc_index, query_start, tile_rows, 0)
                key_doc = lax.dynamic_slice_in_dim(doc_index, key_start, tile_rows, 0)
                allowed = (query_doc[:, None] == key_doc[None, :]) & (key_pos[None, :] <= query_pos[:, None])
                query_term, key_term, value_term = pair_terms(query_rows, grad_rows, norm_rows, delta_rows, allowed, k_block, v_block, scaling)
                query_old = lax.dynamic_slice_in_dim(query_acc, query_start, tile_rows, 0)
                query_acc = lax.dynamic_update_slice_in_dim(query_acc, query_old + query_term.reshape(tile_rows, group_count * HEAD_SIZE), query_start, 0)
                key_old = lax.dynamic_slice_in_dim(key_acc, key_start, tile_rows, 0)
                key_acc = lax.dynamic_update_slice_in_dim(key_acc, key_old + key_term, key_start, 0)
                value_old = lax.dynamic_slice_in_dim(value_acc, key_start, tile_rows, 0)
                value_acc = lax.dynamic_update_slice_in_dim(value_acc, value_old + value_term, key_start, 0)
                return (query_acc, key_acc, value_acc)

            def skipped(state):
                return state
            return lax.cond(needed, compute, skipped, running)
        initial = (jnp.zeros((every_row_set, group_count * HEAD_SIZE), jnp.float32), jnp.zeros((every_row_set, HEAD_SIZE), jnp.float32), jnp.zeros((every_row_set, HEAD_SIZE), jnp.float32))
        query_acc, key_acc, value_acc = lax.fori_loop(0, tile_count * tile_count, visit, initial)
        return (query_acc * scaling, key_acc * scaling, value_acc)
    query_all, key_everything, value_everything = lax.map(one_head, (query_per_head, gradient_per_head, norm_per_head, delta_per_head, key_per_head, value_per_head))
    q_grad = query_all.transpose(1, 0, 2).reshape(every_row_set, QUERY_HEADS * HEAD_SIZE)
    key_gradient = key_everything.transpose(1, 0, 2).reshape(every_row_set, KEY_VALUE_HEADS * HEAD_SIZE)
    value_gradient = value_everything.transpose(1, 0, 2).reshape(every_row_set, KEY_VALUE_HEADS * HEAD_SIZE)
    return (q_grad, key_gradient, value_gradient)
```

```python
import functools
import math

import jax
import jax.numpy as jnp
from jax import lax
from jax.experimental import pallas as pl
from jax.experimental.pallas import tpu as pltpu
from jax.sharding import PartitionSpec as P

AXES = ("wide", "head")
LOG2E = math.log2(math.e)


def shifted(block, shards, by):
    pairs = [(i, i + by) for i in range(shards) if 0 <= i + by < shards]
    return lax.ppermute(block, AXES, pairs)


def attention_kernel(reach, tile, scaling, first_ref, *refs):
    q_ref, g_ref, o_ref, k_ref, v_ref, norm_ref, start_ref = refs[:7]
    earlier = refs[7 : 7 + reach]
    dq_ref, own_ref = refs[-8 - reach : -6 - reach]
    sent = refs[-6 - reach : -6]
    k_win, v_win, dk_win, dv_win, dq_acc, delta_ref = refs[-6:]
    rows, size = k_ref.shape
    groups = q_ref.shape[1] // size
    own = reach * rows
    for j in range(reach):
        k_win[j * rows : (j + 1) * rows] = earlier[j][0]
        v_win[j * rows : (j + 1) * rows] = earlier[j][1]
    k_win[own:] = k_ref[...]
    v_win[own:] = v_ref[...]
    dk_win[:own] = jnp.zeros((own, size), jnp.float32)
    dv_win[:own] = jnp.zeros((own, size), jnp.float32)
    dq_acc[...] = jnp.zeros_like(dq_acc)
    for a in range(groups):
        cut = slice(a * size, (a + 1) * size)
        product = g_ref[:, cut].astype(jnp.float32) * o_ref[:, cut].astype(jnp.float32)
        delta_ref[a : a + 1, :] = jnp.sum(product.T, axis=0, keepdims=True)
    nt = (((1,), (1,)), ((), ()))

    def step(t, carry):
        at = pl.ds(pl.multiple_of(t * tile, tile), tile)
        k_tile = k_win[at, :]
        v_tile = v_win[at, :]
        k_turned = k_tile.T
        key_at = lax.broadcasted_iota(jnp.int32, (tile, rows), 0) + t * tile
        query_at = lax.broadcasted_iota(jnp.int32, (tile, rows), 1) + own
        allowed = (key_at >= start_ref[...]) & (key_at <= query_at)
        dk = jnp.zeros((tile, size), jnp.float32)
        dv = jnp.zeros((tile, size), jnp.float32)
        for a in range(groups):
            q = q_ref[:, a * size : (a + 1) * size]
            g = g_ref[:, a * size : (a + 1) * size]
            s = lax.dot_general(k_tile, q, nt, preferred_element_type=jnp.float32)
            p = jnp.where(
                allowed, jnp.exp2(s * (scaling * LOG2E) - norm_ref[a : a + 1, :]), 0.0
            )
            dp = lax.dot_general(v_tile, g, nt, preferred_element_type=jnp.float32)
            ds = (p * (dp - delta_ref[a : a + 1, :])).astype(jnp.bfloat16)
            dv += jnp.dot(p.astype(jnp.bfloat16), g, preferred_element_type=jnp.float32)
            dk += jnp.dot(ds, q, preferred_element_type=jnp.float32)
            dq_acc[a] += jnp.dot(k_turned, ds, preferred_element_type=jnp.float32)
        dk_win[at, :] = dk * scaling
        dv_win[at, :] = dv
        return carry

    lax.fori_loop(first_ref[0], (own + rows) // tile, step, 0)
    for a in range(groups):
        dq_ref[:, a * size : (a + 1) * size] = dq_acc[a].T * scaling
    own_ref[0] = dk_win[own:]
    own_ref[1] = dv_win[own:]
    for j in range(reach):
        sent[j][0] = dk_win[j * rows : (j + 1) * rows].astype(jnp.bfloat16)
        sent[j][1] = dv_win[j * rows : (j + 1) * rows].astype(jnp.bfloat16)


def attention(first, q, g, o, k, v, norm, start, earlier, dq, at, heads, kv_heads):
    rows, width = q.shape
    reach = len(earlier)
    size = k.shape[1] // kv_heads
    groups = width // k.shape[1]
    tile = min(128, rows)
    scaling = 1.0 / math.sqrt(size)
    here = lambda h, first: (0, h + at)
    pair = pl.BlockSpec((2, rows, size), lambda h, first: (0, 0, h))
    wide = pl.BlockSpec((rows, groups * size), here)
    flat = pl.BlockSpec((groups, rows), lambda h, first: (h + at, 0))
    window = (reach + 1) * rows
    flops = 10 * heads * groups * rows * size * window * 6 // 10
    spec = pltpu.PrefetchScalarGridSpec(
        num_scalar_prefetch=1,
        grid=(heads,),
        in_specs=[
            wide,
            wide,
            wide,
            pl.BlockSpec((rows, size), here),
            pl.BlockSpec((rows, size), here),
            flat,
            pl.BlockSpec((1, rows), lambda h, first: (0, 0)),
        ]
        + [pair] * reach
        + [pl.BlockSpec(memory_space=pl.ANY)] * len(dq),
        out_specs=[wide, pair] + [pair] * reach,
        scratch_shapes=[
            pltpu.VMEM((window, size), jnp.bfloat16),
            pltpu.VMEM((window, size), jnp.bfloat16),
            pltpu.VMEM((window, size), jnp.float32),
            pltpu.VMEM((window, size), jnp.float32),
            pltpu.VMEM((groups, size, rows), jnp.float32),
            pltpu.VMEM((groups, rows), jnp.float32),
        ],
    )
    return pl.pallas_call(
        functools.partial(attention_kernel, reach, tile, scaling),
        grid_spec=spec,
        out_shape=[
            jax.ShapeDtypeStruct((rows, width), jnp.float32),
            jax.ShapeDtypeStruct((2, rows, heads * size), jnp.float32),
        ]
        + [jax.ShapeDtypeStruct((2, rows, heads * size), jnp.bfloat16)] * reach,
        input_output_aliases={8 + reach: 0} if dq else {},
        compiler_params=pltpu.CompilerParams(
            dimension_semantics=("arbitrary",), vmem_limit_bytes=40 << 20
        ),
        cost_estimate=pl.CostEstimate(
            flops=flops,
            bytes_accessed=heads * groups * rows * size * 8,
            transcendentals=heads * groups * rows * window,
        ),
    )(first, q, g, o, k, v, norm, start, *earlier, *dq)


def on_device(shards, splits, queries, keys, values, out_rows, output_gradient, log_norm_rows, doc_lengths):
    rows, width = queries.shape
    query_heads = log_norm_rows.shape[1]
    size = width // query_heads
    kv_heads = keys.shape[1] // size
    reach = shards // 8 - 1
    shard = lax.axis_index(AXES)
    window_start = (shard - reach) * rows
    ends = jnp.cumsum(doc_lengths)
    starts = ends - doc_lengths
    position = shard * rows + jnp.arange(rows, dtype=jnp.int32)
    start = jnp.max(
        jnp.where(starts[None, :] <= position[:, None], starts[None, :], 0), axis=1
    )
    start = (start - window_start).astype(jnp.int32)
    tile = min(128, rows)
    first = (start[0] // tile).reshape(1).astype(jnp.int32)
    start = start.reshape(1, rows)
    norm = (log_norm_rows * LOG2E).T
    heads = kv_heads // splits
    part = heads * size
    arrived = []
    for n in range(splits):
        cut = slice(n * part, (n + 1) * part)
        block = jnp.stack([keys[:, cut], values[:, cut]])
        arrived.append([shifted(block, shards, reach - j) for j in range(reach)])
    dq = ()
    sums = []
    for n in range(splits):
        out = attention(
            first, queries, output_gradient, out_rows, keys, values, norm, start,
            arrived[n], dq, n * heads, heads, kv_heads,
        )
        dq = (out[0],)
        total = out[1]
        for j in range(reach):
            total = total + shifted(out[2 + j], shards, j - reach).astype(jnp.float32)
        sums.append(total)
    total = jnp.concatenate(sums, axis=2)
    return (dq[0], total[0], total[1])


def solution(mesh):
    shards = mesh.shape["wide"] * mesh.shape["head"]
    rows = P(AXES, None)
    return jax.shard_map(
        functools.partial(on_device, shards, 4),
        mesh=mesh,
        in_specs=(rows,) * 6 + (P(),),
        out_specs=(rows,) * 3,
        check_vma=False,
    )
```

```python
import functools
import math

import jax
import jax.numpy as jnp
from jax import lax
from jax.experimental import pallas as pl
from jax.experimental.pallas import tpu as pltpu
from jax.sharding import PartitionSpec as P

AXES = ("wide", "head")
LOG2E = math.log2(math.e)


def shifted(block, shards, by):
    pairs = [(i, i + by) for i in range(shards) if 0 <= i + by < shards]
    return lax.ppermute(block, AXES, pairs)


def attention_kernel(reach, lanes, tile, scaling, count_ref, *refs):
    pieces = reach.bit_length()
    q_ref, g_ref, o_ref, k_ref, v_ref, norm_ref, start_ref = refs[:7]
    earlier = refs[7 : 7 + pieces]
    scratch = refs[-11:]
    k_win, v_win, dk_win, dv_win, q_all, g_all, dq_acc, norm_all, delta_all, bias, turned = scratch
    dq_ref, own_ref = refs[-13 - pieces : -11 - pieces]
    sent = refs[-11 - pieces : -11]
    rows, size = k_ref.shape
    groups = q_ref.shape[1] // size
    halves = rows // lanes
    own = tile + reach * rows
    top = tile // lanes
    limit = bias.shape[1]
    nt = (((1,), (1,)), ((), ()))

    @pl.when(pl.program_id(0) == 0)
    def _():
        k_win[:tile] = jnp.zeros((tile, size), jnp.bfloat16)
        v_win[:tile] = jnp.zeros((tile, size), jnp.bfloat16)
        for half in range(halves):
            end = own + (half + 1) * lanes
            for i in range(limit):
                key_at = lax.broadcasted_iota(jnp.int32, (tile, lanes), 0) + (end - (i + 1) * tile)
                query_at = lax.broadcasted_iota(jnp.int32, (tile, lanes), 1) + (end - lanes)
                start = start_ref[:, half * lanes : (half + 1) * lanes] + tile
                allowed = (key_at >= start) & (key_at <= query_at)
                bias[half, i] = jnp.where(allowed, 0.0, -1e30)

    at = own
    for piece in range(pieces):
        length = earlier[piece].shape[1]
        at = at - length
        k_win[at : at + length] = earlier[piece][0]
        v_win[at : at + length] = earlier[piece][1]
    k_win[own:] = k_ref[...]
    v_win[own:] = v_ref[...]
    dk_win[...] = jnp.zeros_like(dk_win)
    dv_win[...] = jnp.zeros_like(dv_win)
    dq_acc[...] = jnp.zeros_like(dq_acc)
    for a in range(groups):
        cut = slice(a * size, (a + 1) * size)
        product = g_ref[:, cut].astype(jnp.float32) * o_ref[:, cut].astype(jnp.float32)
        delta = jnp.sum(product.T, axis=0, keepdims=True)
        for half in range(halves):
            to = slice(a * lanes, (a + 1) * lanes)
            here = slice(half * lanes, (half + 1) * lanes)
            q_all[half, to] = q_ref[here, cut]
            g_all[half, to] = g_ref[here, cut]
            norm_all[half, :, to] = norm_ref[a : a + 1, here]
            delta_all[half, :, to] = delta[:, here]
    span = top * lanes if groups % top == 0 else lanes

    for half in range(halves):
        end = own + (half + 1) * lanes

        def step(i, carry):
            first = pl.multiple_of(end - (i + 1) * tile, lanes)
            at = pl.ds(first, tile)
            k_tile = k_win[at, :]
            v_tile = v_win[at, :]
            masked = jnp.concatenate([bias[half, i]] * (span // lanes), axis=1)
            lows = []
            for part in range(groups * lanes // span):
                cut = slice(part * span, (part + 1) * span)
                s = lax.dot_general(k_tile, q_all[half, cut], nt, preferred_element_type=jnp.float32)
                p = jnp.exp2(s * (scaling * LOG2E) - norm_all[half, :, cut] + masked)
                dp = lax.dot_general(v_tile, g_all[half, cut], nt, preferred_element_type=jnp.float32)
                ds = (p * (dp - delta_all[half, :, cut])).astype(jnp.bfloat16)
                lows.append((p.astype(jnp.bfloat16), ds))
            p_low = jnp.concatenate([low[0] for low in lows], axis=1)
            ds_low = jnp.concatenate([low[1] for low in lows], axis=1)
            dv_win[at, :] += jnp.dot(p_low, g_all[half], preferred_element_type=jnp.float32)
            dk_win[at, :] += jnp.dot(ds_low, q_all[half], preferred_element_type=jnp.float32)
            dq_acc[half] += jnp.dot(k_tile.T, ds_low, preferred_element_type=jnp.float32)
            return carry

        lax.fori_loop(0, count_ref[half], step, 0)
    for half in range(halves):
        for a in range(groups):
            here = slice(half * lanes, (half + 1) * lanes)
            turn = dq_acc[half, :, a * lanes : (a + 1) * lanes].T
            dq_ref[here, a * size : (a + 1) * size] = turn * scaling
    own_ref[0] = dk_win[own:] * scaling
    own_ref[1] = dv_win[own:]
    at = own
    for piece in range(pieces):
        length = earlier[piece].shape[1]
        at = at - length
        sent[piece][0] = (dk_win[at : at + length] * scaling).astype(jnp.bfloat16)
        sent[piece][1] = dv_win[at : at + length].astype(jnp.bfloat16)


def attention(count, q, g, o, k, v, norm, start, earlier, dq, at, heads, kv_heads, lanes, tile):
    rows, width = q.shape
    pieces = len(earlier)
    reach = (1 << pieces) - 1
    size = k.shape[1] // kv_heads
    groups = width // k.shape[1]
    halves = rows // lanes
    scaling = 1.0 / math.sqrt(size)
    here = lambda h, count: (0, h + at)
    pair = lambda n: pl.BlockSpec((2, n, size), lambda h, count: (0, 0, h))
    wide = pl.BlockSpec((rows, groups * size), here)
    flat = pl.BlockSpec((groups, rows), lambda h, count: (h + at, 0))
    window = (reach + 1) * rows
    lengths = [block.shape[1] for block in earlier]
    limit = pl.cdiv(window, tile)
    spec = pltpu.PrefetchScalarGridSpec(
        num_scalar_prefetch=1,
        grid=(heads,),
        in_specs=[
            wide,
            wide,
            wide,
            pl.BlockSpec((rows, size), here),
            pl.BlockSpec((rows, size), here),
            flat,
            pl.BlockSpec((1, rows), lambda h, count: (0, 0)),
        ]
        + [pair(n) for n in lengths]
        + [pl.BlockSpec(memory_space=pl.ANY)] * len(dq),
        out_specs=[wide, pair(rows)] + [pair(n) for n in lengths],
        scratch_shapes=[
            pltpu.VMEM((tile + window, size), jnp.bfloat16),
            pltpu.VMEM((tile + window, size), jnp.bfloat16),
            pltpu.VMEM((tile + window, size), jnp.float32),
            pltpu.VMEM((tile + window, size), jnp.float32),
            pltpu.VMEM((halves, groups * lanes, size), jnp.bfloat16),
            pltpu.VMEM((halves, groups * lanes, size), jnp.bfloat16),
            pltpu.VMEM((halves, size, groups * lanes), jnp.float32),
            pltpu.VMEM((halves, 1, groups * lanes), jnp.float32),
            pltpu.VMEM((halves, 1, groups * lanes), jnp.float32),
            pltpu.VMEM((halves, limit, tile, lanes), jnp.float32),
            pltpu.VMEM((size, tile), jnp.bfloat16),
        ],
    )
    return pl.pallas_call(
        functools.partial(attention_kernel, reach, lanes, tile, scaling),
        grid_spec=spec,
        out_shape=[
            jax.ShapeDtypeStruct((rows, width), jnp.float32),
            jax.ShapeDtypeStruct((2, rows, heads * size), jnp.float32),
        ]
        + [jax.ShapeDtypeStruct((2, n, heads * size), jnp.bfloat16) for n in lengths],
        input_output_aliases={8 + pieces: 0} if dq else {},
        compiler_params=pltpu.CompilerParams(
            dimension_semantics=("arbitrary",), vmem_limit_bytes=40 << 20
        ),
        cost_estimate=pl.CostEstimate(
            flops=10 * heads * groups * rows * size * window,
            bytes_accessed=heads * groups * rows * size * 8,
            transcendentals=heads * groups * rows * window,
        ),
    )(count, q, g, o, k, v, norm, start, *earlier, *dq)


def on_device(shards, splits, queries, keys, values, out_rows, output_gradient, log_norm_rows, doc_lengths):
    rows, width = queries.shape
    query_heads = log_norm_rows.shape[1]
    size = width // query_heads
    kv_heads = keys.shape[1] // size
    reach = shards // 8 - 1
    shard = lax.axis_index(AXES)
    window_start = (shard - reach) * rows
    ends = jnp.cumsum(doc_lengths)
    starts = ends - doc_lengths
    position = shard * rows + jnp.arange(rows, dtype=jnp.int32)
    start = jnp.max(
        jnp.where(starts[None, :] <= position[:, None], starts[None, :], 0), axis=1
    )
    start = (start - window_start).astype(jnp.int32)
    lanes = min(128, rows)
    tile = 2 * lanes
    halves = rows // lanes
    ends_of = reach * rows + lanes * (1 + jnp.arange(halves, dtype=jnp.int32))
    count = ((ends_of - start[::lanes] + tile - 1) // tile).astype(jnp.int32)
    start = start.reshape(1, rows)
    norm = (log_norm_rows * LOG2E).T
    heads = kv_heads // splits
    part = heads * size
    pieces = reach.bit_length()
    arrived = []
    for n in range(splits):
        cut = slice(n * part, (n + 1) * part)
        block = jnp.stack([keys[:, cut], values[:, cut]])
        got = []
        for d in range(pieces):
            got.append(shifted(block, shards, 1 << d))
            block = jnp.concatenate([got[-1], block], axis=1)
        arrived.append(got)
    dq = ()
    sums = []
    for n in range(splits):
        out = attention(
            count, queries, output_gradient, out_rows, keys, values, norm, start,
            arrived[n], dq, n * heads, heads, kv_heads, lanes, tile,
        )
        dq = (out[0],)
        window = list(out[1:])
        for d in reversed(range(pieces)):
            back = shifted(window.pop(), shards, -(1 << d)).astype(jnp.float32)
            at = back.shape[1]
            for e in range(len(window)):
                at = at - window[e].shape[1]
                piece = back[:, at : at + window[e].shape[1]]
                window[e] = (window[e].astype(jnp.float32) + piece).astype(window[e].dtype)
        sums.append(window[0])
    total = jnp.concatenate(sums, axis=2)
    return (dq[0], total[0], total[1])


def solution(mesh):
    shards = mesh.shape["wide"] * mesh.shape["head"]
    rows = P(AXES, None)
    return jax.shard_map(
        functools.partial(on_device, shards, 2),
        mesh=mesh,
        in_specs=(rows,) * 6 + (P(),),
        out_specs=(rows,) * 3,
        check_vma=False,
    )
```

```python
import functools
import math

import jax
import jax.numpy as jnp
from jax import lax
from jax.experimental import pallas as pl
from jax.experimental.pallas import tpu as pltpu
from jax.sharding import PartitionSpec as P

AXES = ("wide", "head")
LOG2E = math.log2(math.e)


MESH = pl.DeviceIdType.MESH


def attention_kernel(reach, lanes, tile, scaling, sizes, *refs):
    pieces = reach.bit_length()
    q_ref, g_ref, o_ref, k_hbm, v_hbm, norm_ref, start_ref, dq_ref, dk_ref, dv_ref = refs[:10]
    kv, sent, landed, dk_win, dv_win, q_all, g_all, dq_acc, norm_all, delta_all, bias = refs[10:21]
    load_sem, in_send, in_recv, out_send, out_recv = refs[21:]
    rows = k_hbm.shape[0]
    groups = norm_ref.shape[0]
    size = q_ref.shape[1] // groups
    heads = k_hbm.shape[1] // size
    halves = rows // lanes
    own = reach * rows
    length = own + lanes
    full = length // tile
    rest = length - full * tile
    nt = (((1,), (1,)), ((), ()))
    head = pl.program_id(0)
    shards = sizes[0] * sizes[1]
    shard = lax.axis_index(AXES[0]) * sizes[1] + lax.axis_index(AXES[1])

    def device(by):
        other = lax.rem(shard + by + shards, shards)
        return (other // sizes[1], lax.rem(other, sizes[1]))

    def cut_of(c):
        return pl.ds(pl.multiple_of(c * size, size), size)

    def gather(d, c):
        n = rows << d
        at = own + rows - n
        return pltpu.make_async_remote_copy(
            src_ref=kv.at[:, pl.ds(at, n), cut_of(c)],
            dst_ref=kv.at[:, pl.ds(at - n, n), cut_of(c)],
            send_sem=in_send.at[d, c],
            recv_sem=in_recv.at[d, c],
            device_id=device(1 << d),
            device_id_type=MESH,
        )

    def back(d, c):
        n = rows << d
        at = own + rows - 2 * n
        return pltpu.make_async_remote_copy(
            src_ref=sent.at[:, pl.ds(at, n), cut_of(c)],
            dst_ref=landed.at[:, pl.ds(at, n), cut_of(c)],
            send_sem=out_send.at[d, c],
            recv_sem=out_recv.at[d, c],
            device_id=device(-(1 << d)),
            device_id_type=MESH,
        )

    def forward(d, c):
        gather(d - 1, c).wait_recv()
        gather(d, c).start()

    def collect(d, c):
        n = rows << d
        at = own + rows - 2 * n
        back(d, c).wait_recv()
        cut = cut_of(c)
        if n > rows:
            near = pl.ds(own + rows - n, n - rows)
            got = landed[:, pl.ds(at, n - rows), cut].astype(jnp.float32)
            sent[:, near, cut] = (sent[:, near, cut].astype(jnp.float32) + got).astype(jnp.bfloat16)
        last = landed[:, pl.ds(at + n - rows, rows), cut].astype(jnp.float32)
        dk_ref[:, cut] += last[0]
        dv_ref[:, cut] += last[1]
        if d > 0:
            back(d - 1, c).start()

    @pl.when(head == 0)
    def _():
        barrier = pltpu.get_barrier_semaphore()
        for d in range(pieces):
            for by in (1 << d, -(1 << d)):
                pl.semaphore_signal(barrier, inc=1, device_id=device(by), device_id_type=MESH)
        loads = [
            pltpu.make_async_copy(ref, kv.at[n, pl.ds(own, rows)], load_sem.at[n])
            for n, ref in enumerate((k_hbm, v_hbm))
        ]
        for load in loads:
            load.start()
        for load in loads:
            load.wait()
        pl.semaphore_wait(barrier, 2 * pieces)
        for c in range(heads):
            gather(0, c).start()
        for half in range(halves):
            end = own + (half + 1) * lanes
            for i in range(bias.shape[1]):
                key_at = lax.broadcasted_iota(jnp.int32, (tile, lanes), 0) + (end - (i + 1) * tile)
                query_at = lax.broadcasted_iota(jnp.int32, (tile, lanes), 1) + (end - lanes)
                start = start_ref[:, half * lanes : (half + 1) * lanes]
                allowed = (key_at >= start) & (key_at <= query_at)
                bias[half, i] = jnp.where(allowed, 0.0, -1e30)
        for d in range(1, pieces):
            for c in range(min(pieces - d, heads)):
                forward(d, c)

    for d in range(1, pieces):
        ahead = head + pieces - d

        @pl.when(ahead < heads)
        def _():
            forward(d, ahead)

    dk_win[...] = jnp.zeros_like(dk_win)
    dv_win[...] = jnp.zeros_like(dv_win)
    dq_acc[...] = jnp.zeros_like(dq_acc)
    for a in range(groups):
        cut = slice(a * size, (a + 1) * size)
        product = g_ref[:, cut].astype(jnp.float32) * o_ref[:, cut].astype(jnp.float32)
        delta = jnp.sum(product.T, axis=0, keepdims=True)
        for half in range(halves):
            to = slice(a * lanes, (a + 1) * lanes)
            here = slice(half * lanes, (half + 1) * lanes)
            q_all[half, to] = q_ref[here, cut]
            g_all[half, to] = g_ref[here, cut]
            norm_all[half, :, to] = norm_ref[a : a + 1, here]
            delta_all[half, :, to] = delta[:, here]
    span = 2 * lanes if groups % 2 == 0 else lanes
    gather(pieces - 1, head).wait_recv()
    mine = cut_of(head)

    for half in range(halves):
        end = own + (half + 1) * lanes

        def terms(first, count, i):
            at = pl.ds(first, count)
            k_tile = kv[0, at, mine]
            v_tile = kv[1, at, mine]
            masked = bias[half, i][tile - count :]
            masked = jnp.concatenate([masked] * (span // lanes), axis=1)
            lows = []
            for part in range(groups * lanes // span):
                cut = slice(part * span, (part + 1) * span)
                s = lax.dot_general(k_tile, q_all[half, cut], nt, preferred_element_type=jnp.float32)
                p = jnp.exp2(s * (scaling * LOG2E) - norm_all[half, :, cut] + masked)
                dp = lax.dot_general(v_tile, g_all[half, cut], nt, preferred_element_type=jnp.float32)
                ds = (p * (dp - delta_all[half, :, cut])).astype(jnp.bfloat16)
                lows.append((p.astype(jnp.bfloat16), ds))
            p_low = jnp.concatenate([low[0] for low in lows], axis=1)
            ds_low = jnp.concatenate([low[1] for low in lows], axis=1)
            dv_win[at, :] += jnp.dot(p_low, g_all[half], preferred_element_type=jnp.float32)
            dk_win[at, :] += jnp.dot(ds_low, q_all[half], preferred_element_type=jnp.float32)
            dq_acc[half] += jnp.dot(k_tile.T, ds_low, preferred_element_type=jnp.float32)

        def step(i, carry):
            terms(pl.multiple_of(end - (i + 1) * tile, lanes), tile, i)
            return carry

        lax.fori_loop(0, full, step, 0)
        if rest:
            terms(end - length, rest, full)
    dk_ref[:, mine] = dk_win[own:] * scaling
    dv_ref[:, mine] = dv_win[own:]
    sent[0, pl.ds(0, own), mine] = (dk_win[:own] * scaling).astype(jnp.bfloat16)
    sent[1, pl.ds(0, own), mine] = dv_win[:own].astype(jnp.bfloat16)
    for half in range(halves):
        for a in range(groups):
            here = slice(half * lanes, (half + 1) * lanes)
            turn = dq_acc[half, :, a * lanes : (a + 1) * lanes].T
            dq_ref[here, a * size : (a + 1) * size] = turn * scaling
    back(pieces - 1, head).start()
    for d in range(pieces):
        behind = head - (pieces - d)

        @pl.when(behind >= 0)
        def _():
            collect(d, behind)

    @pl.when(head == heads - 1)
    def _():
        for late in range(1, pieces + 1):
            for d in range(pieces):
                c = heads - 1 + late - (pieces - d)
                if 0 <= c < heads:
                    collect(d, c)
        for d in range(pieces):
            for c in range(heads):
                gather(d, c).wait_send()
                back(d, c).wait_send()


def attention(q, g, o, k, v, norm, start, sizes, reach):
    rows, width = q.shape
    pieces = reach.bit_length()
    groups = width // k.shape[1]
    heads = norm.shape[0] // groups
    size = k.shape[1] // heads
    lanes = min(128, rows)
    tile = 2 * lanes
    halves = rows // lanes
    window = (reach + 1) * rows
    wide = pl.BlockSpec((rows, groups * size), lambda h: (0, h))
    whole = pl.BlockSpec(k.shape, lambda h: (0, 0))
    here = pl.BlockSpec(memory_space=pl.ANY)
    copies = pltpu.SemaphoreType.DMA((pieces, heads))
    return pl.pallas_call(
        functools.partial(attention_kernel, reach, lanes, tile, 1.0 / math.sqrt(size), sizes),
        grid=(heads,),
        in_specs=[
            wide,
            wide,
            wide,
            here,
            here,
            pl.BlockSpec((groups, rows), lambda h: (h, 0)),
            pl.BlockSpec((1, rows), lambda h: (0, 0)),
        ],
        out_specs=[wide, whole, whole],
        scratch_shapes=[
            pltpu.VMEM((2, window, k.shape[1]), jnp.bfloat16),
            pltpu.VMEM((2, reach * rows, k.shape[1]), jnp.bfloat16),
            pltpu.VMEM((2, reach * rows, k.shape[1]), jnp.bfloat16),
            pltpu.VMEM((window, size), jnp.float32),
            pltpu.VMEM((window, size), jnp.float32),
            pltpu.VMEM((halves, groups * lanes, size), jnp.bfloat16),
            pltpu.VMEM((halves, groups * lanes, size), jnp.bfloat16),
            pltpu.VMEM((halves, size, groups * lanes), jnp.float32),
            pltpu.VMEM((halves, 1, groups * lanes), jnp.float32),
            pltpu.VMEM((halves, 1, groups * lanes), jnp.float32),
            pltpu.VMEM((halves, pl.cdiv(reach * rows + lanes, tile), tile, lanes), jnp.float32),
            pltpu.SemaphoreType.DMA((2,)),
            copies,
            copies,
            copies,
            copies,
        ],
        out_shape=[
            jax.ShapeDtypeStruct((rows, width), jnp.float32),
            jax.ShapeDtypeStruct(k.shape, jnp.float32),
            jax.ShapeDtypeStruct(k.shape, jnp.float32),
        ],
        compiler_params=pltpu.CompilerParams(
            dimension_semantics=("arbitrary",),
            vmem_limit_bytes=56 << 20,
            collective_id=0,
            has_side_effects=True,
        ),
    )(q, g, o, k, v, norm, start)


def on_device(sizes, queries, keys, values, out_rows, output_gradient, log_norm_rows, doc_lengths):
    rows = queries.shape[0]
    shards = sizes[0] * sizes[1]
    reach = shards // 8 - 1
    shard = lax.axis_index(AXES)
    starts = jnp.cumsum(doc_lengths) - doc_lengths
    position = shard * rows + jnp.arange(rows, dtype=jnp.int32)
    start = jnp.max(
        jnp.where(starts[None, :] <= position[:, None], starts[None, :], 0), axis=1
    )
    start = (start - (shard - reach) * rows).astype(jnp.int32).reshape(1, rows)
    norm = (log_norm_rows * LOG2E).T
    return tuple(
        attention(
            queries, output_gradient, out_rows, keys, values, norm, start, sizes, reach
        )
    )


def solution(mesh):
    sizes = (mesh.shape["wide"], mesh.shape["head"])
    rows = P(AXES, None)
    return jax.shard_map(
        functools.partial(on_device, sizes),
        mesh=mesh,
        in_specs=(rows,) * 6 + (P(),),
        out_specs=(rows,) * 3,
        check_vma=False,
    )
```

```python
import functools
import math

import jax
import jax.numpy as jnp
from jax import lax
from jax.experimental import pallas as pl
from jax.experimental.pallas import tpu as pltpu
from jax.sharding import PartitionSpec as P

AXES = ("wide", "head")
LOG2E = math.log2(math.e)


MESH = pl.DeviceIdType.MESH


def attention_kernel(reach, lanes, tile, scaling, sizes, *refs):
    pieces = reach.bit_length()
    q_ref, g_ref, o_ref, k_hbm, v_hbm, norm_ref, start_ref, dq_ref, dk_ref, dv_ref = refs[:10]
    kv, sent, landed, dk_win, dv_win, q_all, g_all, dq_acc, norm_all, delta_all, bias = refs[10:21]
    load_sem, in_send, in_recv, out_send, out_recv = refs[21:]
    rows = k_hbm.shape[0]
    groups = norm_ref.shape[0]
    size = q_ref.shape[1] // groups
    heads = k_hbm.shape[1] // size
    halves = rows // lanes
    own = reach * rows
    length = own + lanes
    full = length // tile
    rest = length - full * tile
    nt = (((1,), (1,)), ((), ()))
    head = pl.program_id(0)
    lead = pieces + 1
    shards = sizes[0] * sizes[1]
    shard = lax.axis_index(AXES[0]) * sizes[1] + lax.axis_index(AXES[1])

    def device(by):
        other = lax.rem(shard + by + shards, shards)
        return (other // sizes[1], lax.rem(other, sizes[1]))

    def cut_of(c):
        return pl.ds(pl.multiple_of(c * size, size), size)

    def gather(d, c):
        n = rows << d
        at = own + rows - n
        return pltpu.make_async_remote_copy(
            src_ref=kv.at[:, pl.ds(at, n), cut_of(c)],
            dst_ref=kv.at[:, pl.ds(at - n, n), cut_of(c)],
            send_sem=in_send.at[d, c],
            recv_sem=in_recv.at[d, c],
            device_id=device(1 << d),
            device_id_type=MESH,
        )

    def back(d, c):
        n = rows << d
        at = own + rows - 2 * n
        return pltpu.make_async_remote_copy(
            src_ref=sent.at[:, pl.ds(at, n), cut_of(c)],
            dst_ref=landed.at[:, pl.ds(at, n), cut_of(c)],
            send_sem=out_send.at[d, c],
            recv_sem=out_recv.at[d, c],
            device_id=device(-(1 << d)),
            device_id_type=MESH,
        )

    def forward(d, c):
        gather(d - 1, c).wait_recv()
        gather(d, c).start()

    def collect(d, c):
        n = rows << d
        at = own + rows - 2 * n
        back(d, c).wait_recv()
        cut = cut_of(c)
        if n > rows:
            near = pl.ds(own + rows - n, n - rows)
            got = landed[:, pl.ds(at, n - rows), cut].astype(jnp.float32)
            sent[:, near, cut] = (sent[:, near, cut].astype(jnp.float32) + got).astype(jnp.bfloat16)
        last = landed[:, pl.ds(at + n - rows, rows), cut].astype(jnp.float32)
        dk_ref[:, cut] += last[0]
        dv_ref[:, cut] += last[1]
        if d > 0:
            back(d - 1, c).start()

    @pl.when(head == 0)
    def _():
        barrier = pltpu.get_barrier_semaphore()
        for d in range(pieces):
            for by in (1 << d, -(1 << d)):
                pl.semaphore_signal(barrier, inc=1, device_id=device(by), device_id_type=MESH)
        loads = [
            pltpu.make_async_copy(ref, kv.at[n, pl.ds(own, rows)], load_sem.at[n])
            for n, ref in enumerate((k_hbm, v_hbm))
        ]
        for load in loads:
            load.start()
        for load in loads:
            load.wait()
        pl.semaphore_wait(barrier, 2 * pieces)
        for c in range(min(lead, heads)):
            gather(0, c).start()
        for half in range(halves):
            end = own + (half + 1) * lanes
            for i in range(bias.shape[1]):
                key_at = lax.broadcasted_iota(jnp.int32, (tile, lanes), 0) + (end - (i + 1) * tile)
                query_at = lax.broadcasted_iota(jnp.int32, (tile, lanes), 1) + (end - lanes)
                start = start_ref[:, half * lanes : (half + 1) * lanes]
                allowed = (key_at >= start) & (key_at <= query_at)
                bias[half, i] = jnp.where(allowed, 0.0, -1e30)
    dk_win[...] = jnp.zeros_like(dk_win)
    dv_win[...] = jnp.zeros_like(dv_win)
    dq_acc[...] = jnp.zeros_like(dq_acc)
    for a in range(groups):
        cut = slice(a * size, (a + 1) * size)
        product = g_ref[:, cut].astype(jnp.float32) * o_ref[:, cut].astype(jnp.float32)
        delta = jnp.sum(product.T, axis=0, keepdims=True)
        for half in range(halves):
            to = slice(a * lanes, (a + 1) * lanes)
            here = slice(half * lanes, (half + 1) * lanes)
            q_all[half, to] = q_ref[here, cut]
            g_all[half, to] = g_ref[here, cut]
            norm_all[half, :, to] = norm_ref[a : a + 1, here]
            delta_all[half, :, to] = delta[:, here]
    span = 2 * lanes if groups % 2 == 0 else lanes
    mine = cut_of(head)

    @pl.when(head == 0)
    def _():
        for d in range(1, pieces):
            for c in range(min(pieces - d, heads)):
                forward(d, c)

    def tiles(half, near):
        end = own + (half + 1) * lanes
        reached = min(full, ((half + 1) * lanes + rows) // tile)

        def terms(first, count, i):
            at = pl.ds(first, count)
            k_tile = kv[0, at, mine]
            v_tile = kv[1, at, mine]
            masked = bias[half, i][tile - count :]
            masked = jnp.concatenate([masked] * (span // lanes), axis=1)
            lows = []
            for part in range(groups * lanes // span):
                cut = slice(part * span, (part + 1) * span)
                s = lax.dot_general(k_tile, q_all[half, cut], nt, preferred_element_type=jnp.float32)
                p = jnp.exp2(s * (scaling * LOG2E) - norm_all[half, :, cut] + masked)
                dp = lax.dot_general(v_tile, g_all[half, cut], nt, preferred_element_type=jnp.float32)
                ds = (p * (dp - delta_all[half, :, cut])).astype(jnp.bfloat16)
                lows.append((p.astype(jnp.bfloat16), ds))
            p_low = jnp.concatenate([low[0] for low in lows], axis=1)
            ds_low = jnp.concatenate([low[1] for low in lows], axis=1)
            dv_win[at, :] += jnp.dot(p_low, g_all[half], preferred_element_type=jnp.float32)
            dk_win[at, :] += jnp.dot(ds_low, q_all[half], preferred_element_type=jnp.float32)
            dq_acc[half] += jnp.dot(k_tile.T, ds_low, preferred_element_type=jnp.float32)

        def step(i, carry):
            terms(pl.multiple_of(end - (i + 1) * tile, lanes), tile, i)
            return carry

        if near:
            lax.fori_loop(0, reached, step, 0)
        else:
            lax.fori_loop(reached, full, step, 0)
            if rest:
                terms(end - length, rest, full)

    for half in reversed(range(halves)):
        tiles(half, True)

    @pl.when(head + lead < heads)
    def _():
        gather(0, head + lead).start()

    for d in range(1, pieces):
        ahead = head + pieces - d

        @pl.when(ahead < heads)
        def _():
            forward(d, ahead)

    gather(pieces - 1, head).wait_recv()
    for half in range(halves):
        tiles(half, False)
    dk_ref[:, mine] = dk_win[own:] * scaling
    dv_ref[:, mine] = dv_win[own:]
    sent[0, pl.ds(0, own), mine] = (dk_win[:own] * scaling).astype(jnp.bfloat16)
    sent[1, pl.ds(0, own), mine] = dv_win[:own].astype(jnp.bfloat16)
    for half in range(halves):
        for a in range(groups):
            here = slice(half * lanes, (half + 1) * lanes)
            turn = dq_acc[half, :, a * lanes : (a + 1) * lanes].T
            dq_ref[here, a * size : (a + 1) * size] = turn * scaling
    back(pieces - 1, head).start()
    for d in range(pieces):
        behind = head - (pieces - d)

        @pl.when(behind >= 0)
        def _():
            collect(d, behind)

    @pl.when(head == heads - 1)
    def _():
        for late in range(1, pieces + 1):
            for d in range(pieces):
                c = heads - 1 + late - (pieces - d)
                if 0 <= c < heads:
                    collect(d, c)
        for d in range(pieces):
            for c in range(heads):
                gather(d, c).wait_send()
                back(d, c).wait_send()


def attention(q, g, o, k, v, norm, start, sizes, reach):
    rows, width = q.shape
    pieces = reach.bit_length()
    groups = width // k.shape[1]
    heads = norm.shape[0] // groups
    size = k.shape[1] // heads
    lanes = min(128, rows)
    tile = 2 * lanes
    halves = rows // lanes
    window = (reach + 1) * rows
    wide = pl.BlockSpec((rows, groups * size), lambda h: (0, h))
    whole = pl.BlockSpec(k.shape, lambda h: (0, 0))
    here = pl.BlockSpec(memory_space=pl.ANY)
    copies = pltpu.SemaphoreType.DMA((pieces, heads))
    return pl.pallas_call(
        functools.partial(attention_kernel, reach, lanes, tile, 1.0 / math.sqrt(size), sizes),
        grid=(heads,),
        in_specs=[
            wide,
            wide,
            wide,
            here,
            here,
            pl.BlockSpec((groups, rows), lambda h: (h, 0)),
            pl.BlockSpec((1, rows), lambda h: (0, 0)),
        ],
        out_specs=[wide, whole, whole],
        scratch_shapes=[
            pltpu.VMEM((2, window, k.shape[1]), jnp.bfloat16),
            pltpu.VMEM((2, reach * rows, k.shape[1]), jnp.bfloat16),
            pltpu.VMEM((2, reach * rows, k.shape[1]), jnp.bfloat16),
            pltpu.VMEM((window, size), jnp.float32),
            pltpu.VMEM((window, size), jnp.float32),
            pltpu.VMEM((halves, groups * lanes, size), jnp.bfloat16),
            pltpu.VMEM((halves, groups * lanes, size), jnp.bfloat16),
            pltpu.VMEM((halves, size, groups * lanes), jnp.float32),
            pltpu.VMEM((halves, 1, groups * lanes), jnp.float32),
            pltpu.VMEM((halves, 1, groups * lanes), jnp.float32),
            pltpu.VMEM((halves, pl.cdiv(reach * rows + lanes, tile), tile, lanes), jnp.float32),
            pltpu.SemaphoreType.DMA((2,)),
            copies,
            copies,
            copies,
            copies,
        ],
        out_shape=[
            jax.ShapeDtypeStruct((rows, width), jnp.float32),
            jax.ShapeDtypeStruct(k.shape, jnp.float32),
            jax.ShapeDtypeStruct(k.shape, jnp.float32),
        ],
        compiler_params=pltpu.CompilerParams(
            dimension_semantics=("arbitrary",),
            vmem_limit_bytes=56 << 20,
            collective_id=0,
            has_side_effects=True,
        ),
    )(q, g, o, k, v, norm, start)


def on_device(sizes, queries, keys, values, out_rows, output_gradient, log_norm_rows, doc_lengths):
    rows = queries.shape[0]
    shards = sizes[0] * sizes[1]
    reach = shards // 8 - 1
    shard = lax.axis_index(AXES)
    starts = jnp.cumsum(doc_lengths) - doc_lengths
    position = shard * rows + jnp.arange(rows, dtype=jnp.int32)
    start = jnp.max(
        jnp.where(starts[None, :] <= position[:, None], starts[None, :], 0), axis=1
    )
    start = (start - (shard - reach) * rows).astype(jnp.int32).reshape(1, rows)
    norm = (log_norm_rows * LOG2E).T
    return tuple(
        attention(
            queries, output_gradient, out_rows, keys, values, norm, start, sizes, reach
        )
    )


def solution(mesh):
    sizes = (mesh.shape["wide"], mesh.shape["head"])
    rows = P(AXES, None)
    return jax.shard_map(
        functools.partial(on_device, sizes),
        mesh=mesh,
        in_specs=(rows,) * 6 + (P(),),
        out_specs=(rows,) * 3,
        check_vma=False,
    )
```

```python
import functools
import math

import jax
import jax.numpy as jnp
from jax import lax
from jax.experimental import pallas as pl
from jax.experimental.pallas import tpu as pltpu
from jax.sharding import PartitionSpec as P

AXES = ("wide", "head")
LOG2E = math.log2(math.e)


MESH = pl.DeviceIdType.MESH


def attention_kernel(reach, lanes, tile, scaling, sizes, *refs):
    pieces = reach.bit_length()
    q_ref, g_ref, o_ref, k_hbm, v_hbm, norm_ref, start_ref, dq_ref, dk_ref, dv_ref = refs[:10]
    kv, sent, landed, dk_win, dv_win, q_all, g_all, dq_acc, norm_all, delta_all, bias = refs[10:21]
    load_sem, in_send, in_recv, out_send, out_recv = refs[21:]
    rows = k_hbm.shape[0]
    groups = norm_ref.shape[0]
    size = q_ref.shape[1] // groups
    heads = k_hbm.shape[1] // size
    halves = rows // lanes
    own = reach * rows
    length = own + lanes
    full = length // tile
    rest = length - full * tile
    nt = (((1,), (1,)), ((), ()))
    head = pl.program_id(0)
    lead = pieces + 1
    shards = sizes[0] * sizes[1]
    shard = lax.axis_index(AXES[0]) * sizes[1] + lax.axis_index(AXES[1])

    def device(by):
        other = lax.rem(shard + by + shards, shards)
        return (other // sizes[1], lax.rem(other, sizes[1]))

    def cut_of(c):
        return pl.ds(pl.multiple_of(c * size, size), size)

    def gather(d, c):
        n = rows << d
        at = own + rows - n
        return pltpu.make_async_remote_copy(
            src_ref=kv.at[:, pl.ds(at, n), cut_of(c)],
            dst_ref=kv.at[:, pl.ds(at - n, n), cut_of(c)],
            send_sem=in_send.at[d, c],
            recv_sem=in_recv.at[d, c],
            device_id=device(1 << d),
            device_id_type=MESH,
        )

    def back(d, c):
        n = rows << d
        at = own + rows - 2 * n
        return pltpu.make_async_remote_copy(
            src_ref=sent.at[:, pl.ds(at, n), cut_of(c)],
            dst_ref=landed.at[:, pl.ds(at, n), cut_of(c)],
            send_sem=out_send.at[d, c],
            recv_sem=out_recv.at[d, c],
            device_id=device(-(1 << d)),
            device_id_type=MESH,
        )

    def forward(d, c):
        gather(d - 1, c).wait_recv()
        gather(d, c).start()

    def collect(d, c):
        n = rows << d
        at = own + rows - 2 * n
        back(d, c).wait_recv()
        cut = cut_of(c)
        if n > rows:
            near = pl.ds(own + rows - n, n - rows)
            got = landed[:, pl.ds(at, n - rows), cut].astype(jnp.float32)
            sent[:, near, cut] = (sent[:, near, cut].astype(jnp.float32) + got).astype(jnp.bfloat16)
        last = landed[:, pl.ds(at + n - rows, rows), cut].astype(jnp.float32)
        dk_ref[:, cut] += last[0]
        dv_ref[:, cut] += last[1]
        if d > 0:
            back(d - 1, c).start()

    @pl.when(head == 0)
    def _():
        barrier = pltpu.get_barrier_semaphore()
        for d in range(pieces):
            for by in (1 << d, -(1 << d)):
                pl.semaphore_signal(barrier, inc=1, device_id=device(by), device_id_type=MESH)
        loads = [
            pltpu.make_async_copy(ref, kv.at[n, pl.ds(own, rows)], load_sem.at[n])
            for n, ref in enumerate((k_hbm, v_hbm))
        ]
        for load in loads:
            load.start()
        for load in loads:
            load.wait()
        pl.semaphore_wait(barrier, 2 * pieces)
        for c in range(min(lead, heads)):
            gather(0, c).start()
        for half in range(halves):
            end = own + (half + 1) * lanes
            for i in range(bias.shape[1]):
                key_at = lax.broadcasted_iota(jnp.int32, (tile, lanes), 0) + (end - (i + 1) * tile)
                query_at = lax.broadcasted_iota(jnp.int32, (tile, lanes), 1) + (end - lanes)
                start = start_ref[:, half * lanes : (half + 1) * lanes]
                allowed = (key_at >= start) & (key_at <= query_at)
                bias[half, i] = jnp.where(allowed, 0.0, -1e30)
    dk_win[...] = jnp.zeros_like(dk_win)
    dv_win[...] = jnp.zeros_like(dv_win)
    dq_acc[...] = jnp.zeros_like(dq_acc)
    for a in range(groups):
        cut = slice(a * size, (a + 1) * size)
        product = g_ref[:, cut].astype(jnp.float32) * o_ref[:, cut].astype(jnp.float32)
        delta = jnp.sum(product.T, axis=0, keepdims=True)
        for half in range(halves):
            to = slice(a * lanes, (a + 1) * lanes)
            here = slice(half * lanes, (half + 1) * lanes)
            q_all[half, to] = q_ref[here, cut]
            g_all[half, to] = g_ref[here, cut]
            norm_all[half, :, to] = norm_ref[a : a + 1, here]
            delta_all[half, :, to] = delta[:, here]
    span = 2 * lanes if groups % 2 == 0 else lanes
    mine = cut_of(head)

    @pl.when(head == 0)
    def _():
        for d in range(1, pieces):
            for c in range(min(pieces - d, heads)):
                forward(d, c)

    def tiles(half, near):
        end = own + (half + 1) * lanes
        reached = min(full, ((half + 1) * lanes + rows) // tile)

        def terms(first, count, i):
            at = pl.ds(first, count)
            k_tile = kv[0, at, mine]
            v_tile = kv[1, at, mine]
            masked = bias[half, i][tile - count :]
            masked = jnp.concatenate([masked] * (span // lanes), axis=1)
            lows = []
            for part in range(groups * lanes // span):
                cut = slice(part * span, (part + 1) * span)
                s = lax.dot_general(k_tile, q_all[half, cut], nt, preferred_element_type=jnp.float32)
                p = jnp.exp2(s * (scaling * LOG2E) - norm_all[half, :, cut] + masked)
                dp = lax.dot_general(v_tile, g_all[half, cut], nt, preferred_element_type=jnp.float32)
                ds = (p * (dp - delta_all[half, :, cut])).astype(jnp.bfloat16)
                lows.append((p.astype(jnp.bfloat16), ds))
            p_low = jnp.concatenate([low[0] for low in lows], axis=1)
            ds_low = jnp.concatenate([low[1] for low in lows], axis=1)
            dv_win[at, :] += jnp.dot(p_low, g_all[half], preferred_element_type=jnp.float32)
            dk_win[at, :] += jnp.dot(ds_low, q_all[half], preferred_element_type=jnp.float32)
            dq_acc[half] += jnp.dot(k_tile.T, ds_low, preferred_element_type=jnp.float32)

        def step(i, carry):
            terms(pl.multiple_of(end - (i + 1) * tile, lanes), tile, i)
            return carry

        if near:
            lax.fori_loop(0, reached, step, 0)
        else:
            lax.fori_loop(reached, full, step, 0)
            if rest:
                terms(end - length, rest, full)

    @pl.when(head == 0)
    def _():
        for half in reversed(range(halves)):
            tiles(half, True)

    @pl.when(head + lead < heads)
    def _():
        gather(0, head + lead).start()

    for d in range(1, pieces):
        ahead = head + pieces - d

        @pl.when(ahead < heads)
        def _():
            forward(d, ahead)

    gather(pieces - 1, head).wait_recv()
    for half in range(halves):
        tiles(half, False)
    far = own - rows
    sent[0, pl.ds(0, far), mine] = (dk_win[:far] * scaling).astype(jnp.bfloat16)
    sent[1, pl.ds(0, far), mine] = dv_win[:far].astype(jnp.bfloat16)
    back(pieces - 1, head).start()

    @pl.when(head > 0)
    def _():
        for half in range(halves):
            tiles(half, True)

    dk_ref[:, mine] = dk_win[own:] * scaling
    dv_ref[:, mine] = dv_win[own:]
    sent[0, pl.ds(far, rows), mine] = (dk_win[far:own] * scaling).astype(jnp.bfloat16)
    sent[1, pl.ds(far, rows), mine] = dv_win[far:own].astype(jnp.bfloat16)
    for half in range(halves):
        for a in range(groups):
            here = slice(half * lanes, (half + 1) * lanes)
            turn = dq_acc[half, :, a * lanes : (a + 1) * lanes].T
            dq_ref[here, a * size : (a + 1) * size] = (turn * scaling).astype(dq_ref.dtype)
    for d in range(pieces):
        behind = head - (pieces - d)

        @pl.when(behind >= 0)
        def _():
            collect(d, behind)

    @pl.when(head == heads - 1)
    def _():
        for late in range(1, pieces + 1):
            for d in range(pieces):
                c = heads - 1 + late - (pieces - d)
                if 0 <= c < heads:
                    collect(d, c)
        for d in range(pieces):
            for c in range(heads):
                gather(d, c).wait_send()
                back(d, c).wait_send()


def attention(q, g, o, k, v, norm, start, sizes, reach):
    rows, width = q.shape
    pieces = reach.bit_length()
    groups = width // k.shape[1]
    heads = norm.shape[0] // groups
    size = k.shape[1] // heads
    lanes = min(128, rows)
    tile = 2 * lanes
    halves = rows // lanes
    window = (reach + 1) * rows
    wide = pl.BlockSpec((rows, groups * size), lambda h: (0, h))
    whole = pl.BlockSpec(k.shape, lambda h: (0, 0))
    here = pl.BlockSpec(memory_space=pl.ANY)
    copies = pltpu.SemaphoreType.DMA((pieces, heads))
    return pl.pallas_call(
        functools.partial(attention_kernel, reach, lanes, tile, 1.0 / math.sqrt(size), sizes),
        grid=(heads,),
        in_specs=[
            wide,
            wide,
            wide,
            here,
            here,
            pl.BlockSpec((groups, rows), lambda h: (h, 0)),
            pl.BlockSpec((1, rows), lambda h: (0, 0)),
        ],
        out_specs=[wide, whole, whole],
        scratch_shapes=[
            pltpu.VMEM((2, window, k.shape[1]), jnp.bfloat16),
            pltpu.VMEM((2, reach * rows, k.shape[1]), jnp.bfloat16),
            pltpu.VMEM((2, reach * rows, k.shape[1]), jnp.bfloat16),
            pltpu.VMEM((window, size), jnp.float32),
            pltpu.VMEM((window, size), jnp.float32),
            pltpu.VMEM((halves, groups * lanes, size), jnp.bfloat16),
            pltpu.VMEM((halves, groups * lanes, size), jnp.bfloat16),
            pltpu.VMEM((halves, size, groups * lanes), jnp.float32),
            pltpu.VMEM((halves, 1, groups * lanes), jnp.float32),
            pltpu.VMEM((halves, 1, groups * lanes), jnp.float32),
            pltpu.VMEM((halves, pl.cdiv(reach * rows + lanes, tile), tile, lanes), jnp.float32),
            pltpu.SemaphoreType.DMA((2,)),
            copies,
            copies,
            copies,
            copies,
        ],
        out_shape=[
            jax.ShapeDtypeStruct((rows, width), jnp.bfloat16),
            jax.ShapeDtypeStruct(k.shape, jnp.float32),
            jax.ShapeDtypeStruct(k.shape, jnp.float32),
        ],
        compiler_params=pltpu.CompilerParams(
            dimension_semantics=("arbitrary",),
            vmem_limit_bytes=56 << 20,
            collective_id=0,
            has_side_effects=True,
        ),
    )(q, g, o, k, v, norm, start)


def on_device(sizes, queries, keys, values, out_rows, output_gradient, log_norm_rows, doc_lengths):
    rows = queries.shape[0]
    shards = sizes[0] * sizes[1]
    reach = shards // 8 - 1
    shard = lax.axis_index(AXES)
    starts = jnp.cumsum(doc_lengths) - doc_lengths
    position = shard * rows + jnp.arange(rows, dtype=jnp.int32)
    start = jnp.max(
        jnp.where(starts[None, :] <= position[:, None], starts[None, :], 0), axis=1
    )
    start = (start - (shard - reach) * rows).astype(jnp.int32).reshape(1, rows)
    norm = (log_norm_rows * LOG2E).T
    dq, dk, dv = attention(
        queries, output_gradient, out_rows, keys, values, norm, start, sizes, reach
    )
    return (dq.astype(jnp.float32), dk, dv)


def solution(mesh):
    sizes = (mesh.shape["wide"], mesh.shape["head"])
    rows = P(AXES, None)
    return jax.shard_map(
        functools.partial(on_device, sizes),
        mesh=mesh,
        in_specs=(rows,) * 6 + (P(),),
        out_specs=(rows,) * 3,
        check_vma=False,
    )
```
